32 devices in a mesh: table: 8 (over z, y), dense: 4 (over x, core).
Axes of the slice: x: 2, y: 2, z: 4, core: 2. Of those that a mesh axis runs over, the one named last changes fastest.
Arguments:
- table: float32 [8192, 128], P('table'), may hold values from -3 to 3
- slot_rows: int32 [4, 2560, 4], P('dense', 'table'), may hold values from 0 to 1023, as said below
- slot_mult: int32 [4, 2560, 4], P('dense', 'table'), may hold values from 0 to 3, as said below
- slot_cell: int32 [4, 2560], P('dense', 'table'), may hold values from 0 to 3328, as said below
- dense_in: bfloat16 [4, 1024, 128], P('dense', 'table'), may hold values from -6 to 6
- down_w: bfloat16 [256, 3456], P('table'), may hold values from -0.109375 to 0.109375
- up_w: bfloat16 [256, 3456], P('table'), may hold values from -0.375 to 0.375
- bias: float32 [3456], replicated, may hold values from -3 to 3
- grad_out: bfloat16 [4, 1024, 3456], P('dense', 'table'), may hold values from -6 to 6
Outputs:
- crossed: bfloat16 [4, 1024, 3456], P('dense', 'table')
- grad_table: float32 [8192, 128], P('table')
- grad_dense: float32 [4, 1024, 128], P('dense', 'table')
- grad_down: float32 [256, 3456], P('table')
- grad_up: float32 [256, 3456], P('table')
- grad_bias: float32 [3456], replicated
The draws below stay inside these ranges and needn't reach their ends.
Inputs may be any that keep to these rules, and one draw needn't show every extreme that they name: `slot_rows`: a local row of the sending shard. `slot_mult`: 0 exactly on empty slots. `slot_cell`: 3328 marks an empty slot; in every replica one owner receives 40 live slots from every sender.
All inputs are finite; a program needn't handle non-finite values.
Results may differ from the reference program's by a relative error of at most 0.0066.
Values may be sent and summed in bfloat16 or wider, within the bound.
No kernel may reach another device: no remote copies, remote signals or barrier semaphores. Data moves between devices by JAX's collectives and lax.ppermute only.
A program may use at most 128 MiB of HBM per device.

```python
import jax
import jax.numpy as jnp
from jax import lax

E = 128
NF = 26
RANK = 256
HOT = 4
BATCH_DEV = 128
ROWS_DEV = 1024
CAP = 40
WIDTH = 3456
SAMPLES = 1024
N_TABLE = 8
N_DENSE = 4


def slot_pattern(key):
    keys = jax.random.split(jax.random.fold_in(key, 7), 5)
    live = jax.random.randint(keys[0], (N_DENSE, N_TABLE, N_TABLE), CAP // 4, CAP + 1)
    busiest = jax.random.randint(keys[1], (N_DENSE, 1, 1), 0, N_TABLE)
    owner = jnp.arange(N_TABLE, dtype=jnp.int32).reshape(1, 1, N_TABLE)
    live = jnp.where(owner == busiest, CAP, live)
    slot = jnp.arange(CAP, dtype=jnp.int32).reshape(1, 1, 1, CAP)
    used = slot < live[..., None]
    cells = jax.random.randint(keys[2], (N_DENSE, N_TABLE, N_TABLE, CAP), 0, BATCH_DEV * NF)
    cells = jnp.where(used, cells, BATCH_DEV * NF)
    rows = jax.random.randint(keys[3], (N_DENSE, N_TABLE, N_TABLE, CAP, HOT), 0, ROWS_DEV)
    mult = jax.random.randint(keys[4], (N_DENSE, N_TABLE, N_TABLE, CAP, HOT), 1, 4)
    mult = jnp.where(used[..., None], mult, 0)
    total = N_TABLE * N_TABLE * CAP
    return (rows.reshape(N_DENSE, total, HOT), mult.reshape(N_DENSE, total, HOT), cells.reshape(N_DENSE, total))


def draw_slot_rows(key, part):
    return slot_pattern(key)[0].astype(jnp.int32)


def draw_slot_mult(key, part):
    return slot_pattern(key)[1].astype(jnp.int32)


def draw_slot_cell(key, part):
    return slot_pattern(key)[2].astype(jnp.int32)


def block_levels(stream_key, extent, pieces, low, high):
    def one(position, parts):
        draws = jax.random.uniform(jax.random.fold_in(jax.random.fold_in(stream_key, 6), position), (parts,), jnp.float32, low / len(pieces), high / len(pieces))
        return jnp.repeat(jnp.exp(draws), extent[position] // parts).reshape((-1,) + (1,) * (len(extent) - position - 1))

    factor_of = one(*pieces[0])
    for cut in pieces[1:]:
        factor_of = factor_of * one(*cut)
    return factor_of


def bell_draw(own_key, shape, width, reach, cuts=(), kind=jnp.bfloat16):
    loudness = block_levels(own_key, shape, cuts, -0.22, 0.18) if cuts else 1.0
    array = jax.random.normal(own_key, shape, jnp.float32) * width * loudness
    return jnp.minimum(jnp.maximum(array, -reach), reach).astype(kind)


def setup_inputs(seed: int = 0) -> dict:
    key_list = jax.random.split(jax.random.key(seed), 10)
    table = bell_draw(key_list[0], (ROWS_DEV * N_TABLE, E), 0.5, 3.0, ((0, 8),), jnp.float32)
    slot_rows = draw_slot_rows(jax.random.fold_in(key_list[9], 71), 0)
    slot_mult = draw_slot_mult(jax.random.fold_in(key_list[9], 71), 0)
    slot_cell = draw_slot_cell(jax.random.fold_in(key_list[9], 71), 0)
    dense_in = bell_draw(key_list[4], (N_DENSE, SAMPLES, E), 1.0, 6.0, ((0, 4), (1, 8)))
    down_w = bell_draw(key_list[5], (RANK, WIDTH), WIDTH ** -0.5, 0.109375, ((0, 8),))
    up_w = bell_draw(key_list[6], (RANK, WIDTH), RANK ** -0.5, 0.375, ((0, 8),))
    bias = bell_draw(key_list[7], (WIDTH,), 0.5, 3.0, (), jnp.float32)
    grad_out = bell_draw(key_list[8], (N_DENSE, SAMPLES, WIDTH), 1.0, 6.0, ((0, 4), (1, 8)))
    return dict(table=table, slot_rows=slot_rows, slot_mult=slot_mult, slot_cell=slot_cell, dense_in=dense_in, down_w=down_w, up_w=up_w, bias=bias, grad_out=grad_out)


def replica(table3, rows, mult, cells, dense_x, down_w, up_w, bias, g_in):
    ncell = BATCH_DEV * NF

    def shard_partial(item):
        shard, shard_rows, shard_mult = item
        picked = jnp.take(shard, shard_rows, axis=0)
        return lax.optimization_barrier(jnp.sum(shard_mult.astype(jnp.float32)[:, :, None] * picked, axis=1))
    partial_value = lax.map(shard_partial, (table3, rows, mult))
    owner = jnp.repeat(jnp.arange(N_TABLE, dtype=jnp.int32), CAP)
    ids = jnp.where(cells < ncell, owner[None, :] * ncell + cells, N_TABLE * ncell).astype(jnp.int32)
    pooled = jax.ops.segment_sum(partial_value.reshape(-1, E), ids.reshape(-1), num_segments=N_TABLE * ncell + 1)
    pooled = pooled[:N_TABLE * ncell].reshape(N_TABLE * BATCH_DEV, NF * E)
    x0 = jnp.concatenate([dense_x.astype(jnp.float32), pooled], axis=1).astype(jnp.bfloat16)
    x0f = x0.astype(jnp.float32)
    low = jnp.dot(x0, down_w.T, preferred_element_type=jnp.float32).astype(jnp.bfloat16)
    up = jnp.dot(low, up_w, preferred_element_type=jnp.float32) + bias
    crossed = (x0f * up + x0f).astype(jnp.bfloat16)
    grad = g_in.astype(jnp.float32)
    gup32 = grad * x0f
    gbias = lax.optimization_barrier(jnp.sum(gup32, axis=0))
    gup = gup32.astype(jnp.bfloat16)
    gupw = jnp.dot(low.T, gup, preferred_element_type=jnp.float32)
    glow = jnp.dot(gup, up_w.T, preferred_element_type=jnp.float32).astype(jnp.bfloat16)
    gdown = jnp.dot(glow.T, x0, preferred_element_type=jnp.float32)
    gx0 = grad * (up + 1.0) + jnp.dot(glow, down_w, preferred_element_type=jnp.float32)
    gdense = gx0[:, :E]
    gpool = jnp.concatenate([gx0[:, E:].reshape(N_TABLE * ncell, E), jnp.zeros((1, E), jnp.float32)], axis=0)
    slot_grad = jnp.take(gpool, ids, axis=0)

    def shard_grad(item):
        shard_rows, shard_mult, grads = item
        terms = shard_mult.astype(jnp.float32)[:, :, None] * grads[:, None, :]
        return jax.ops.segment_sum(terms.reshape(-1, E), shard_rows.reshape(-1), num_segments=ROWS_DEV)
    gtable = lax.map(shard_grad, (rows, mult, slot_grad)).reshape(N_TABLE * ROWS_DEV, E)
    return (crossed, gtable, gdense, gdown, gupw, gbias)

def reference(table, slot_rows, slot_mult, slot_cell, dense_in, down_w, up_w, bias, grad_out):
    per = N_TABLE * CAP
    table3 = table.reshape(N_TABLE, ROWS_DEV, E)
    crossed_all = []
    dense_all = []
    gtable = jnp.zeros((N_TABLE * ROWS_DEV, E), jnp.float32)
    gdown = jnp.zeros((RANK, WIDTH), jnp.float32)
    gupw = jnp.zeros((RANK, WIDTH), jnp.float32)
    gbias = jnp.zeros((WIDTH,), jnp.float32)
    for rep in range(N_DENSE):
        rows = slot_rows[rep].reshape(N_TABLE, per, HOT)
        mult = slot_mult[rep].reshape(N_TABLE, per, HOT)
        cells = slot_cell[rep].reshape(N_TABLE, per)
        out = replica(table3, rows, mult, cells, dense_in[rep], down_w, up_w, bias, grad_out[rep])
        crossed_all.append(out[0])
        gtable = gtable + out[1]
        dense_all.append(out[2])
        gdown = gdown + out[3]
        gupw = gupw + out[4]
        gbias = gbias + out[5]
    return (jnp.stack(crossed_all), gtable, jnp.stack(dense_all), gdown, gupw, gbias)
```

```python
import jax
import jax.numpy as jnp
from jax import lax
from jax.experimental import pallas as pl
from jax.experimental.pallas import tpu as pltpu
from jax.sharding import PartitionSpec as P

E = 128
NF = 26


def local(table, slot_rows, slot_mult, slot_cell, dense_in, down_w, up_w, bias, grad_out):
    batch = dense_in.shape[1]
    ncell = batch * NF
    rows = slot_rows[0]
    mult = slot_mult[0].astype(jnp.float32)
    cells = slot_cell[0]
    picked = jnp.take(table, rows, axis=0)
    partial_value = jnp.sum(mult[:, :, None] * picked, axis=1)
    recv_part, recv_cell = (
        lax.all_to_all(partial_value, "table", split_axis=0, concat_axis=0, tiled=True),
        lax.all_to_all(cells, "table", split_axis=0, concat_axis=0, tiled=True),
    )
    pooled = jax.ops.segment_sum(recv_part, recv_cell, num_segments=ncell + 1)[:ncell]
    pooled = pooled.reshape(batch, NF * E)
    x0 = jnp.concatenate([dense_in[0].astype(jnp.float32), pooled], axis=1).astype(jnp.bfloat16)
    x0f = x0.astype(jnp.float32)
    full_down, full_up = (
        lax.all_gather(down_w, "table", axis=0, tiled=True),
        lax.all_gather(up_w, "table", axis=0, tiled=True),
    )
    low = jnp.einsum("bw,rw->br", x0, full_down, preferred_element_type=jnp.float32).astype(
        jnp.bfloat16
    )
    up = jnp.dot(low, full_up, preferred_element_type=jnp.float32) + bias
    crossed = (x0f * up + x0f).astype(jnp.bfloat16)
    grad = grad_out[0].astype(jnp.float32)
    gup32 = grad * x0f
    gup = gup32.astype(jnp.bfloat16)
    glow = jnp.einsum("bw,rw->br", gup, full_up, preferred_element_type=jnp.float32).astype(
        jnp.bfloat16
    )
    gx0 = grad * (up + 1.0) + jnp.dot(glow, full_down, preferred_element_type=jnp.float32)
    grad_dense = gx0[:, :E]
    gpool = jnp.concatenate([gx0[:, E:].reshape(ncell, E), jnp.zeros((1, E), jnp.float32)], axis=0)
    back_grad = jnp.take(gpool, recv_cell, axis=0)
    slot_grad = lax.all_to_all(back_grad, "table", split_axis=0, concat_axis=0, tiled=True)
    terms = mult[:, :, None] * slot_grad[:, None, :]
    local_table = jax.ops.segment_sum(
        terms.reshape(-1, E), rows.reshape(-1), num_segments=table.shape[0]
    )
    grad_table = lax.psum(local_table, "dense")
    block = low
    share_up = lax.psum_scatter(
        jnp.einsum("br,bw->rw", block, gup, preferred_element_type=jnp.float32),
        "table",
        scatter_dimension=0,
        tiled=True,
    )
    block = glow
    share_down = lax.psum_scatter(
        jnp.einsum("br,bw->rw", block, x0, preferred_element_type=jnp.float32),
        "table",
        scatter_dimension=0,
        tiled=True,
    )
    grad_up, grad_down = lax.psum((share_up, share_down), "dense")
    grad_bias = lax.psum(jnp.sum(gup32, axis=0), ("table", "dense"))
    return (crossed[None], grad_table, grad_dense[None], grad_down, grad_up, grad_bias)


def _up(n, m):
    return -(-n // m) * m


def _dot(a, b, ca, cb):
    return lax.dot_general(
        a, b, (((ca,), (cb,)), ((), ())), preferred_element_type=jnp.float32
    )


def _call(body, outs, scratch=(), flops=0, moved=0, name=None):
    space = pl.BlockSpec(memory_space=pltpu.VMEM)

    def run(*args):
        return pl.pallas_call(
            body,
            out_shape=[jax.ShapeDtypeStruct(s, t) for s, t in outs],
            in_specs=[space] * len(args),
            out_specs=[space] * len(outs),
            scratch_shapes=list(scratch),
            cost_estimate=pl.CostEstimate(flops=flops, bytes_accessed=moved, transcendentals=0),
            compiler_params=pltpu.CompilerParams(vmem_limit_bytes=60 * 1024 * 1024),
            name=name,
        )(*args)

    return run


def fast(sizes, table, slot_rows, slot_mult, slot_cell, dense_in, down_w, up_w, bias, grad_out):
    T, D = sizes
    TZ, DX = T // 2, D // 2
    batch, width = grad_out.shape[1], grad_out.shape[2]
    nb = width // E
    bq = -(-nb // D)
    qw = bq * E
    padw = D * qw
    r = down_w.shape[0]
    rank = r * T
    nrow = table.shape[0]
    hot = slot_rows.shape[2]
    cap = slot_rows.shape[1] // T
    cp = _up(cap + 8, 16)
    ns = T * cp
    bf, f32 = jnp.bfloat16, jnp.float32
    axes = ("table", "dense")

    def swap(v, k=0, j=0, dx=0, dc=0):
        t_off, d_off = k * 2 + j, dx * 2 + dc
        pairs = [
            (t * D + d, (t ^ t_off) * D + (d ^ d_off)) for t in range(T) for d in range(D)
        ]
        return lax.ppermute(v, axes, pairs)

    t_id = lax.axis_index("table")
    d_id = lax.axis_index("dense")
    core = lax.rem(d_id, 2)

    mine = jnp.where(core == 0, down_w, up_w)
    wz = [mine] + [swap(mine, k=k) for k in range(1, TZ)]
    wy = [swap(w, j=1) for w in wz]
    own_w = [w for pair in zip(wz, wy) for w in pair]
    other_w = [swap(w, dc=1) for w in own_w]

    ints = jnp.concatenate(
        [slot_rows[0], slot_mult[0], slot_cell[0][:, None]], axis=1
    ).reshape(T, cap, 2 * hot + 1)
    ints = jnp.transpose(ints, (2, 0, 1))
    bits = T.bit_length() - 1
    ints = ints.reshape((2 * hot + 1,) + (2,) * bits + (cap,))
    for i in range(bits):
        bit = lax.rem(lax.div(t_id, 1 << (bits - 1 - i)), 2)
        ints = jnp.where(bit == 1, jnp.flip(ints, axis=1 + i), ints)
    ints = ints.reshape(2 * hot + 1, T, cap)
    slots = jnp.pad(ints[: 2 * hot], ((0, 0), (0, 0), (0, cp - cap))).reshape(2 * hot, ns)
    cells = jnp.pad(ints[2 * hot], ((0, 0), (0, 128 - cap)), constant_values=batch * NF)

    def embed(slots_ref, cell_ref, tab_ref, mt_ref, *z_refs):
        step = 128
        for c in range(nrow // step):
            rows = lax.broadcasted_iota(jnp.int32, (step, ns), 0) + c * step
            acc = jnp.zeros((step, ns), f32)
            for h in range(hot):
                m = slots_ref[hot + h : hot + h + 1, :].astype(f32)
                acc = acc + jnp.where(rows == slots_ref[h : h + 1, :], m, 0.0)
            mt_ref[c * step : (c + 1) * step, :] = acc.astype(bf)
        tab = tab_ref[...]
        hi = tab.astype(bf)
        lo = (tab - hi.astype(f32)).astype(bf)
        mt = mt_ref[...]
        part = _dot(mt, hi, 0, 0) + _dot(mt, lo, 0, 0)
        cell = cell_ref[...].astype(f32)
        bag = jnp.floor((cell + 0.5) * (1.0 / NF))
        feat = cell - bag * NF
        for k in range(TZ):
            for j in range(2):
                b = k * 2 + j
                block = jnp.concatenate(
                    [
                        part[b * cp : b * cp + cap],
                        bag[b : b + 1],
                        feat[b : b + 1],
                        jnp.zeros((cp - cap - 2, E), f32),
                    ],
                    axis=0,
                )
                z_refs[k][j] = block.astype(bf)

    mt, *zs = _call(
        embed,
        [((nrow, ns), bf)] + [((2, cp, E), bf)] * TZ,
        flops=4 * nrow * ns * E,
        moved=4 * nrow * E + 2 * nrow * ns,
        name="embed",
    )(slots, cells, table)
    zr = [zs[0]] + [swap(zs[k], k=k) for k in range(1, TZ)]
    yr = swap(jnp.stack([z[1] for z in zr]), j=1)

    def pool(*refs):
        z_refs, (y_ref, dense_ref, g_ref) = refs[:TZ], refs[TZ : TZ + 3]
        x0_ref, gup_ref, at_ref, feat_ref, kk_ref, kc_ref, xk_ref, xc_ref = refs[TZ + 3 : TZ + 11]
        r_ref, xp_ref, gp_ref = refs[TZ + 11 :]
        sub = lax.broadcasted_iota(jnp.int32, (cp, E), 0)
        lane = lax.broadcasted_iota(jnp.int32, (cp, E), 1)
        blocks = []
        for k in range(TZ):
            for j in range(2):
                blk = (z_refs[k][0] if j == 0 else y_ref[k]).astype(f32)
                b = k * 2 + j
                diag = sub == lane
                bag = jnp.sum(jnp.where(diag, blk[cap : cap + 1], 0.0), axis=1, keepdims=True)
                feat = jnp.sum(
                    jnp.where(diag, blk[cap + 1 : cap + 2], 0.0), axis=1, keepdims=True
                )
                live = sub[:, :1] < cap
                feat = jnp.where(live, feat, -1.0)
                hit = (bag == lane[:, :].astype(f32)) & live
                at_ref[b * cp : (b + 1) * cp, :] = jnp.where(hit, 1.0, 0.0).astype(bf)
                feat_ref[b * cp : (b + 1) * cp, :] = jnp.broadcast_to(feat, (cp, E))
                blocks.append(blk)
        vals = jnp.concatenate(blocks, axis=0)
        feat = feat_ref[...]
        for f in range(NF):
            r_ref[:, f * E : (f + 1) * E] = jnp.where(feat == f, vals, 0.0).astype(bf)
        pooled = _dot(at_ref[...], r_ref[...], 0, 0)
        xp_ref[:, :E] = dense_ref[...]
        xp_ref[:, E:width] = pooled.astype(bf)
        gp_ref[:, :width] = (
            g_ref[...].astype(f32) * xp_ref[:, :width].astype(f32)
        ).astype(bf)
        if padw > width:
            xp_ref[:, width:] = jnp.zeros((batch, padw - width), bf)
            gp_ref[:, width:] = jnp.zeros((batch, padw - width), bf)
        x0_ref[...] = xp_ref[:, :width]
        gup_ref[...] = gp_ref[:, :width]
        d = lax.axis_index("dense")
        for off, o_ref in ((0, kk_ref), (1, kc_ref), (2, xk_ref), (3, xc_ref)):
            q = jnp.bitwise_xor(d, off)
            sl = pl.ds(pl.multiple_of(q * qw, E), qw)
            o_ref[0] = gp_ref[:, sl]
            o_ref[1] = xp_ref[:, sl]

    x0, gup, at, feat, kk, kc, xk, xc = _call(
        pool,
        [((batch, width), bf)] * 2
        + [((ns, batch), bf), ((ns, E), f32)]
        + [((2, batch, qw), bf)] * 4,
        scratch=[
            pltpu.VMEM((ns, NF * E), bf),
            pltpu.VMEM((batch, padw), bf),
            pltpu.VMEM((batch, padw), bf),
        ],
        flops=2 * batch * ns * NF * E,
        moved=10 * batch * width,
        name="pool",
    )(*zr, yr, dense_in[0], grad_out[0])
    from_core = swap(kc, dc=1)
    far = swap(xc, dc=1)
    from_x = swap(xk, dx=1)
    from_xc = swap(far, dx=1)

    def project(*refs):
        w_refs, (x_ref, g_ref, o_ref, w_scr) = refs[: 2 * T], refs[2 * T :]
        c = lax.rem(lax.axis_index("dense"), 2)
        for which, src_ref in ((0, x_ref), (1, g_ref)):
            for side in range(2):

                @pl.when(c == side)
                def _(which=which, side=side):
                    group = w_refs[:T] if which == side else w_refs[T:]
                    for b in range(T):
                        w_scr[b * r : (b + 1) * r, :] = group[b][...]

            o_ref[:, which * rank : (which + 1) * rank] = _dot(
                src_ref[...], w_scr[...], 1, 1
            ).astype(bf)

    (lg,) = _call(
        project,
        [((batch, 2 * rank), bf)],
        scratch=[pltpu.VMEM((rank, width), bf)],
        flops=4 * batch * rank * width,
        moved=4 * rank * width + 4 * batch * width,
        name="project",
    )(*own_w, *other_w, x0, gup)
    lg_x = swap(lg, dx=1)
    lg_c = swap(lg, dc=1)
    lg_xc = swap(lg_x, dc=1)

    def cross(*refs):
        w_refs = refs[: 2 * T]
        x_ref, g_ref, lg_ref, b_ref, at_ref, f_ref = refs[2 * T : 2 * T + 6]
        cr_ref, gd_ref = refs[2 * T + 6 : 2 * T + 8]
        z_refs = refs[2 * T + 8 : 2 * T + 8 + TZ]
        w_scr, gx_ref = refs[2 * T + 8 + TZ :]
        c = lax.rem(lax.axis_index("dense"), 2)
        for which in (1, 0):
            for side in range(2):

                @pl.when(c == side)
                def _(which=which, side=side):
                    group = w_refs[:T] if which == side else w_refs[T:]
                    for b in range(T):
                        w_scr[b * r : (b + 1) * r, :] = group[b][...]

            half = lg_ref[:, (1 - which) * rank : (2 - which) * rank]
            prod = _dot(half, w_scr[...], 1, 0)
            if which == 1:
                up = prod + b_ref[...]
                x = x_ref[...].astype(f32)
                cr_ref[...] = (x * up + x).astype(bf)
                gx_ref[...] = g_ref[...].astype(f32) * (up + 1.0)
            else:
                gx_ref[...] += prod
        gd_ref[...] = gx_ref[:, :E]
        feat = f_ref[...]
        acc = jnp.zeros((ns, E), f32)
        a = at_ref[...]
        for f in range(NF):
            got = _dot(a, gx_ref[:, (f + 1) * E : (f + 2) * E].astype(bf), 1, 0)
            acc = acc + jnp.where(feat == f, got, 0.0)
        for k in range(TZ):
            for j in range(2):
                b = k * 2 + j
                z_refs[k][j] = acc[b * cp : (b + 1) * cp].astype(bf)

    crossed, gdense, *bz = _call(
        cross,
        [((batch, width), bf), ((batch, E), f32)] + [((2, cp, E), bf)] * TZ,
        scratch=[pltpu.VMEM((rank, width), bf), pltpu.VMEM((batch, width), f32)],
        flops=4 * batch * rank * width,
        moved=4 * rank * width + 6 * batch * width,
        name="cross",
    )(*own_w, *other_w, x0, grad_out[0], lg, bias.reshape(1, width), at, feat)
    bzr = [bz[0]] + [swap(bz[k], k=k) for k in range(1, TZ)]
    byr = swap(jnp.stack([z[1] for z in bzr]), j=1)

    def shares(*refs):
        lgs, acts = refs[:4], refs[4:8]
        us_ref, uk_ref, ds_ref, dk_ref, l_scr, a_scr = refs[8:]
        for i in range(4):
            l_scr[i * batch : (i + 1) * batch, :] = lgs[i][...]
            a_scr[i * batch : (i + 1) * batch, :qw] = acts[i][0]
            a_scr[i * batch : (i + 1) * batch, qw:] = acts[i][1]
        bias_sum = jnp.sum(a_scr[:, :qw].astype(f32), axis=0, keepdims=True)
        rows = [bias_sum[:, i * E : (i + 1) * E] for i in range(bq)]
        extra = jnp.concatenate(rows + [jnp.zeros((r - bq, E), f32)], axis=0).astype(bf)
        gu = _dot(l_scr[:, :rank], a_scr[:, :qw], 0, 0).astype(bf)
        gd = _dot(l_scr[:, rank:], a_scr[:, qw:], 0, 0).astype(bf)
        for k in range(TZ):
            for j, (u_ref, d_ref) in enumerate(((uk_ref, dk_ref), (us_ref, ds_ref))):
                b = k * 2 + j
                u_ref[k, :, :qw] = gu[b * r : (b + 1) * r]
                u_ref[k, :, qw:] = extra
                d_ref[k] = gd[b * r : (b + 1) * r]

    us, uk, ds, dk = _call(
        shares,
        [((TZ, r, qw + E), bf)] * 2 + [((TZ, r, qw), bf)] * 2,
        scratch=[pltpu.VMEM((4 * batch, 2 * rank), bf), pltpu.VMEM((4 * batch, 2 * qw), bf)],
        flops=16 * batch * rank * qw,
        moved=16 * batch * (rank + qw),
        name="shares",
    )(lg, lg_x, lg_c, lg_xc, kk, from_x, from_core, from_xc)

    def pair(*refs):
        keep_ref, got_ref = refs[:2]
        for k in range(TZ):
            s = keep_ref[k].astype(f32) + got_ref[k].astype(f32)
            refs[2 + k][...] = s.astype(bf)

    def reduced(send, keep, name):
        got = swap(send, j=1)
        w = keep.shape[2]
        zs = _call(pair, [((r, w), bf)] * TZ, moved=6 * TZ * r * w, name=name)(keep, got)
        return [zs[0]] + [swap(zs[k], k=k) for k in range(1, TZ)]

    ups = reduced(us, uk, "pair_up")
    downs = reduced(ds, dk, "pair_down")
    last = _up(2, 16)

    def total(terms):
        while len(terms) > 1:
            terms = [a + b for a, b in zip(terms[::2], terms[1::2])]
        return terms[0]

    def finish(*refs):
        o_ref = refs[-1]
        up = total([u[...].astype(f32) for u in refs[:TZ]])
        down = total([d[...].astype(f32) for d in refs[TZ : 2 * TZ]])
        o_ref[:r, :] = up[:, :qw].astype(bf)
        o_ref[r : 2 * r, :] = down.astype(bf)
        row = jnp.concatenate([up[i : i + 1, qw:] for i in range(bq)], axis=1)
        hi = row.astype(bf).astype(f32)
        tail = jnp.concatenate([hi, row - hi, jnp.zeros((last - 2, qw), f32)], axis=0)
        o_ref[2 * r :, :] = tail.astype(bf)

    (fin,) = _call(finish, [((2 * r + last, qw), bf)], moved=8 * r * qw * TZ, name="finish")(
        *ups, *downs
    )
    fin_x = swap(fin, dx=1)
    fin_c = swap(fin, dc=1)
    fin_xc = swap(fin_x, dc=1)

    def spread(*refs):
        ins = refs[:4]
        gd_ref, gu_ref, gb_ref, scr = refs[4:]
        d = lax.axis_index("dense")
        for off, i_ref in zip((0, 2, 1, 3), ins):
            q = jnp.bitwise_xor(d, off)
            scr[:, pl.ds(pl.multiple_of(q * qw, E), qw)] = i_ref[...].astype(f32)
        gu_ref[...] = scr[:r, :width]
        gd_ref[...] = scr[r : 2 * r, :width]
        gb_ref[...] = scr[2 * r : 2 * r + 1, :width] + scr[2 * r + 1 : 2 * r + 2, :width]

    gdown, gup_w, gbias = _call(
        spread,
        [((r, width), f32)] * 2 + [((1, width), f32)],
        scratch=[pltpu.VMEM((2 * r + last, padw), f32)],
        moved=24 * r * width,
        name="spread",
    )(fin, fin_x, fin_c, fin_xc)

    half = nrow // 2

    def scatter(*refs):
        z_refs, (y_ref, mt_ref, keep_ref, send_ref, sg, out) = refs[:TZ], refs[TZ:]
        for k in range(TZ):
            sg[(2 * k) * cp : (2 * k + 1) * cp, :] = z_refs[k][0]
            sg[(2 * k + 1) * cp : (2 * k + 2) * cp, :] = y_ref[k]
        out[...] = _dot(mt_ref[...], sg[...], 1, 0)
        c = lax.rem(lax.axis_index("dense"), 2)
        keep_ref[...] = out[pl.ds(pl.multiple_of(c * half, 8), half), :]
        send_ref[...] = out[pl.ds(pl.multiple_of((1 - c) * half, 8), half), :].astype(bf)

    t_keep, t_send = _call(
        scatter,
        [((half, E), f32), ((half, E), bf)],
        scratch=[pltpu.VMEM((ns, E), bf), pltpu.VMEM((nrow, E), f32)],
        flops=2 * nrow * ns * E,
        moved=2 * nrow * ns,
        name="scatter",
    )(*bzr, byr, mt)
    t_half = (t_keep + swap(t_send, dc=1).astype(f32)).astype(bf)
    t_sum = t_half.astype(f32) + swap(t_half, dx=1).astype(f32)
    t_other = swap(t_sum, dc=1)
    gtable = jnp.where(
        core == 0,
        jnp.concatenate([t_sum, t_other], axis=0),
        jnp.concatenate([t_other, t_sum], axis=0),
    )
    return (crossed[None], gtable, gdense[None], gdown, gup_w, gbias.reshape(width))


def fits(sizes, args):
    T, D = sizes
    table, slot_rows, down_w, grad_out = args[0], args[1], args[5], args[8]
    batch, width = grad_out.shape[1:]
    cap = slot_rows.shape[1] // T
    return (
        D == 4
        and T >= 4
        and T & (T - 1) == 0
        and down_w.shape[0] % 16 == 0
        and batch == E
        and width % E == 0
        and table.shape[0] % E == 0
        and cap % 8 == 0
        and cap <= E
        and -(-(width // E) // D) <= down_w.shape[0]
    )


def solution(mesh):
    placed = (
        P("table", None),
        P("dense", "table", None),
        P("dense", "table", None),
        P("dense", "table"),
        P("dense", "table", None),
        P("table", None),
        P("table", None),
        P(),
        P("dense", "table", None),
    )
    sizes = (mesh.shape["table"], mesh.shape["dense"])

    def step(*args):
        return fast(sizes, *args) if fits(sizes, args) else local(*args)

    return jax.shard_map(
        step,
        mesh=mesh,
        in_specs=placed,
        out_specs=(
            P("dense", "table", None),
            P("table", None),
            P("dense", "table", None),
            P("table", None),
            P("table", None),
            P(),
        ),
        check_vma=False,
    )
```

```python
import jax
import jax.numpy as jnp
from jax import lax
from jax.experimental import pallas as pl
from jax.experimental.pallas import tpu as pltpu
from jax.sharding import PartitionSpec as P

E = 128
NF = 26


def local(table, slot_rows, slot_mult, slot_cell, dense_in, down_w, up_w, bias, grad_out):
    batch = dense_in.shape[1]
    ncell = batch * NF
    rows = slot_rows[0]
    mult = slot_mult[0].astype(jnp.float32)
    cells = slot_cell[0]
    picked = jnp.take(table, rows, axis=0)
    partial_value = jnp.sum(mult[:, :, None] * picked, axis=1)
    recv_part, recv_cell = (
        lax.all_to_all(partial_value, "table", split_axis=0, concat_axis=0, tiled=True),
        lax.all_to_all(cells, "table", split_axis=0, concat_axis=0, tiled=True),
    )
    pooled = jax.ops.segment_sum(recv_part, recv_cell, num_segments=ncell + 1)[:ncell]
    pooled = pooled.reshape(batch, NF * E)
    x0 = jnp.concatenate([dense_in[0].astype(jnp.float32), pooled], axis=1).astype(jnp.bfloat16)
    x0f = x0.astype(jnp.float32)
    full_down, full_up = (
        lax.all_gather(down_w, "table", axis=0, tiled=True),
        lax.all_gather(up_w, "table", axis=0, tiled=True),
    )
    low = jnp.einsum("bw,rw->br", x0, full_down, preferred_element_type=jnp.float32).astype(
        jnp.bfloat16
    )
    up = jnp.dot(low, full_up, preferred_element_type=jnp.float32) + bias
    crossed = (x0f * up + x0f).astype(jnp.bfloat16)
    grad = grad_out[0].astype(jnp.float32)
    gup32 = grad * x0f
    gup = gup32.astype(jnp.bfloat16)
    glow = jnp.einsum("bw,rw->br", gup, full_up, preferred_element_type=jnp.float32).astype(
        jnp.bfloat16
    )
    gx0 = grad * (up + 1.0) + jnp.dot(glow, full_down, preferred_element_type=jnp.float32)
    grad_dense = gx0[:, :E]
    gpool = jnp.concatenate([gx0[:, E:].reshape(ncell, E), jnp.zeros((1, E), jnp.float32)], axis=0)
    back_grad = jnp.take(gpool, recv_cell, axis=0)
    slot_grad = lax.all_to_all(back_grad, "table", split_axis=0, concat_axis=0, tiled=True)
    terms = mult[:, :, None] * slot_grad[:, None, :]
    local_table = jax.ops.segment_sum(
        terms.reshape(-1, E), rows.reshape(-1), num_segments=table.shape[0]
    )
    grad_table = lax.psum(local_table, "dense")
    block = low
    share_up = lax.psum_scatter(
        jnp.einsum("br,bw->rw", block, gup, preferred_element_type=jnp.float32),
        "table",
        scatter_dimension=0,
        tiled=True,
    )
    block = glow
    share_down = lax.psum_scatter(
        jnp.einsum("br,bw->rw", block, x0, preferred_element_type=jnp.float32),
        "table",
        scatter_dimension=0,
        tiled=True,
    )
    grad_up, grad_down = lax.psum((share_up, share_down), "dense")
    grad_bias = lax.psum(jnp.sum(gup32, axis=0), ("table", "dense"))
    return (crossed[None], grad_table, grad_dense[None], grad_down, grad_up, grad_bias)


def _up(n, m):
    return -(-n // m) * m


def _dot(a, b, ca, cb):
    return lax.dot_general(
        a, b, (((ca,), (cb,)), ((), ())), preferred_element_type=jnp.float32
    )


def _call(body, outs, scratch=(), flops=0, moved=0, name=None, mib=8):
    space = pl.BlockSpec(memory_space=pltpu.VMEM)

    def run(*args):
        return pl.pallas_call(
            body,
            out_shape=[jax.ShapeDtypeStruct(s, t) for s, t in outs],
            in_specs=[space] * len(args),
            out_specs=[space] * len(outs),
            scratch_shapes=list(scratch),
            cost_estimate=pl.CostEstimate(flops=flops, bytes_accessed=moved, transcendentals=0),
            compiler_params=pltpu.CompilerParams(vmem_limit_bytes=mib * 1024 * 1024),
            name=name,
        )(*args)

    return run


def fast(sizes, table, slot_rows, slot_mult, slot_cell, dense_in, down_w, up_w, bias, grad_out):
    T, D = sizes
    TZ, DX = T // 2, D // 2
    batch, width = grad_out.shape[1], grad_out.shape[2]
    nb = width // E
    bq = -(-nb // D)
    qw = bq * E
    padw = D * qw
    r = down_w.shape[0]
    rank = r * T
    nrow = table.shape[0]
    hot = slot_rows.shape[2]
    cap = slot_rows.shape[1] // T
    cp = _up(cap + 8, 16)
    ns = T * cp
    bf, f32 = jnp.bfloat16, jnp.float32
    axes = ("table", "dense")

    def swap(v, k=0, j=0, dx=0, dc=0):
        t_off, d_off = k * 2 + j, dx * 2 + dc
        pairs = [
            (t * D + d, (t ^ t_off) * D + (d ^ d_off)) for t in range(T) for d in range(D)
        ]
        return lax.ppermute(v, axes, pairs)

    def second(zs):
        def pick(*refs):
            for k in range(TZ):
                refs[TZ][k] = refs[k][1]

        return _call(pick, [((TZ, cp, E), bf)], name="pick", mib=2)(*zs)[0]

    t_id = lax.axis_index("table")
    d_id = lax.axis_index("dense")
    core = lax.rem(d_id, 2)

    mine = jnp.where(core == 0, down_w, up_w)
    wz = [mine] + [swap(mine, k=k) for k in range(1, TZ)]
    wy = [swap(w, j=1) for w in wz]
    own_w = [w for pair in zip(wz, wy) for w in pair]
    other_w = [swap(w, dc=1) for w in own_w]

    ints = jnp.concatenate(
        [slot_rows[0], slot_mult[0], slot_cell[0][:, None]], axis=1
    ).reshape(T, cap, 2 * hot + 1)
    ints = jnp.transpose(ints, (2, 0, 1))
    bits = T.bit_length() - 1
    ints = ints.reshape((2 * hot + 1,) + (2,) * bits + (cap,))
    for i in range(bits):
        bit = lax.rem(lax.div(t_id, 1 << (bits - 1 - i)), 2)
        ints = jnp.where(bit == 1, jnp.flip(ints, axis=1 + i), ints)
    ints = ints.reshape(2 * hot + 1, T, cap)
    slots = jnp.pad(ints[: 2 * hot], ((0, 0), (0, 0), (0, cp - cap))).reshape(2 * hot, ns)
    cells = jnp.pad(ints[2 * hot], ((0, 0), (0, 128 - cap)), constant_values=batch * NF)

    def embed(slots_ref, cell_ref, tab_ref, mt_ref, *z_refs):
        step = 128
        for c in range(nrow // step):
            rows = lax.broadcasted_iota(jnp.int32, (step, ns), 0) + c * step
            acc = jnp.zeros((step, ns), f32)
            for h in range(hot):
                m = slots_ref[hot + h : hot + h + 1, :].astype(f32)
                acc = acc + jnp.where(rows == slots_ref[h : h + 1, :], m, 0.0)
            mt_ref[c * step : (c + 1) * step, :] = acc.astype(bf)
        tab = tab_ref[...]
        hi = tab.astype(bf)
        lo = (tab - hi.astype(f32)).astype(bf)
        mt = mt_ref[...]
        part = _dot(mt, hi, 0, 0) + _dot(mt, lo, 0, 0)
        cell = cell_ref[...].astype(f32)
        bag = jnp.floor((cell + 0.5) * (1.0 / NF))
        feat = cell - bag * NF
        for k in range(TZ):
            for j in range(2):
                b = k * 2 + j
                block = jnp.concatenate(
                    [
                        part[b * cp : b * cp + cap],
                        bag[b : b + 1],
                        feat[b : b + 1],
                        jnp.zeros((cp - cap - 2, E), f32),
                    ],
                    axis=0,
                )
                z_refs[k][j] = block.astype(bf)

    mt, *zs = _call(
        embed,
        [((nrow, ns), bf)] + [((2, cp, E), bf)] * TZ,
        flops=4 * nrow * ns * E,
        moved=4 * nrow * E + 2 * nrow * ns,
        name="embed",
        mib=10,
    )(slots, cells, table)
    zr = [zs[0]] + [swap(zs[k], k=k) for k in range(1, TZ)]
    yr = swap(second(zr), j=1)

    def pool(*refs):
        z_refs, (y_ref, dense_ref, g_ref) = refs[:TZ], refs[TZ : TZ + 3]
        x0_ref, gup_ref, at_ref, feat_ref, kk_ref, kc_ref, xk_ref, xc_ref = refs[TZ + 3 : TZ + 11]
        r_ref, xp_ref, gp_ref = refs[TZ + 11 :]
        sub = lax.broadcasted_iota(jnp.int32, (cp, E), 0)
        lane = lax.broadcasted_iota(jnp.int32, (cp, E), 1)
        blocks = []
        for k in range(TZ):
            for j in range(2):
                blk = (z_refs[k][0] if j == 0 else y_ref[k]).astype(f32)
                b = k * 2 + j
                diag = sub == lane
                bag = jnp.sum(jnp.where(diag, blk[cap : cap + 1], 0.0), axis=1, keepdims=True)
                feat = jnp.sum(
                    jnp.where(diag, blk[cap + 1 : cap + 2], 0.0), axis=1, keepdims=True
                )
                live = sub[:, :1] < cap
                feat = jnp.where(live, feat, -1.0)
                hit = (bag == lane[:, :].astype(f32)) & live
                at_ref[b * cp : (b + 1) * cp, :] = jnp.where(hit, 1.0, 0.0).astype(bf)
                feat_ref[b * cp : (b + 1) * cp, :] = jnp.broadcast_to(feat, (cp, E))
                blocks.append(blk)
        vals = jnp.concatenate(blocks, axis=0)
        feat = feat_ref[...]
        for f in range(NF):
            r_ref[:, f * E : (f + 1) * E] = jnp.where(feat == f, vals, 0.0).astype(bf)
        pooled = _dot(at_ref[...], r_ref[...], 0, 0)
        xp_ref[:, :E] = dense_ref[...]
        xp_ref[:, E:width] = pooled.astype(bf)
        gp_ref[:, :width] = (
            g_ref[...].astype(f32) * xp_ref[:, :width].astype(f32)
        ).astype(bf)
        if padw > width:
            xp_ref[:, width:] = jnp.zeros((batch, padw - width), bf)
            gp_ref[:, width:] = jnp.zeros((batch, padw - width), bf)
        x0_ref[...] = xp_ref[:, :width]
        gup_ref[...] = gp_ref[:, :width]
        d = lax.axis_index("dense")
        for off, o_ref in ((0, kk_ref), (1, kc_ref), (2, xk_ref), (3, xc_ref)):
            q = jnp.bitwise_xor(d, off)
            sl = pl.ds(pl.multiple_of(q * qw, E), qw)
            o_ref[0] = gp_ref[:, sl]
            o_ref[1] = xp_ref[:, sl]

    x0, gup, at, feat, kk, kc, xk, xc = _call(
        pool,
        [((batch, width), bf)] * 2
        + [((ns, batch), bf), ((ns, E), f32)]
        + [((2, batch, qw), bf)] * 4,
        scratch=[
            pltpu.VMEM((ns, NF * E), bf),
            pltpu.VMEM((batch, padw), bf),
            pltpu.VMEM((batch, padw), bf),
        ],
        flops=2 * batch * ns * NF * E,
        moved=10 * batch * width,
        name="pool",
        mib=14,
    )(*zr, yr, dense_in[0], grad_out[0])
    from_core = swap(kc, dc=1)
    far = swap(xc, dc=1)
    from_x = swap(xk, dx=1)
    from_xc = swap(far, dx=1)

    def project(*refs):
        w_refs, (x_ref, g_ref, o_ref, w_scr) = refs[: 2 * T], refs[2 * T :]
        c = lax.rem(lax.axis_index("dense"), 2)
        for which, src_ref in ((0, x_ref), (1, g_ref)):
            for side in range(2):

                @pl.when(c == side)
                def _(which=which, side=side):
                    group = w_refs[:T] if which == side else w_refs[T:]
                    for b in range(T):
                        w_scr[b * r : (b + 1) * r, :] = group[b][...]

            o_ref[:, which * rank : (which + 1) * rank] = _dot(
                src_ref[...], w_scr[...], 1, 1
            ).astype(bf)

    (lg,) = _call(
        project,
        [((batch, 2 * rank), bf)],
        scratch=[pltpu.VMEM((rank, width), bf)],
        flops=4 * batch * rank * width,
        moved=4 * rank * width + 4 * batch * width,
        name="project",
        mib=10,
    )(*own_w, *other_w, x0, gup)
    lg_x = swap(lg, dx=1)
    lg_c = swap(lg, dc=1)
    lg_xc = swap(lg_x, dc=1)

    def cross(*refs):
        w_refs = refs[: 2 * T]
        x_ref, g_ref, lg_ref, b_ref, at_ref, f_ref = refs[2 * T : 2 * T + 6]
        cr_ref, gd_ref = refs[2 * T + 6 : 2 * T + 8]
        z_refs = refs[2 * T + 8 : 2 * T + 8 + TZ]
        w_scr, gx_ref = refs[2 * T + 8 + TZ :]
        c = lax.rem(lax.axis_index("dense"), 2)
        for which in (1, 0):
            for side in range(2):

                @pl.when(c == side)
                def _(which=which, side=side):
                    group = w_refs[:T] if which == side else w_refs[T:]
                    for b in range(T):
                        w_scr[b * r : (b + 1) * r, :] = group[b][...]

            half = lg_ref[:, (1 - which) * rank : (2 - which) * rank]
            prod = _dot(half, w_scr[...], 1, 0)
            if which == 1:
                up = prod + b_ref[...]
                x = x_ref[...].astype(f32)
                cr_ref[...] = (x * up + x).astype(bf)
                gx_ref[...] = g_ref[...].astype(f32) * (up + 1.0)
            else:
                gx_ref[...] += prod
        gd_ref[...] = gx_ref[:, :E]
        feat = f_ref[...]
        acc = jnp.zeros((ns, E), f32)
        a = at_ref[...]
        for f in range(NF):
            got = _dot(a, gx_ref[:, (f + 1) * E : (f + 2) * E].astype(bf), 1, 0)
            acc = acc + jnp.where(feat == f, got, 0.0)
        for k in range(TZ):
            for j in range(2):
                b = k * 2 + j
                z_refs[k][j] = acc[b * cp : (b + 1) * cp].astype(bf)

    crossed, gdense, *bz = _call(
        cross,
        [((batch, width), bf), ((batch, E), f32)] + [((2, cp, E), bf)] * TZ,
        scratch=[pltpu.VMEM((rank, width), bf), pltpu.VMEM((batch, width), f32)],
        flops=4 * batch * rank * width,
        moved=4 * rank * width + 6 * batch * width,
        name="cross",
        mib=16,
    )(*own_w, *other_w, x0, grad_out[0], lg, bias.reshape(1, width), at, feat)
    bzr = [bz[0]] + [swap(bz[k], k=k) for k in range(1, TZ)]
    byr = swap(second(bzr), j=1)

    def shares(*refs):
        lgs, acts = refs[:4], refs[4:8]
        us_ref, uk_ref, ds_ref, dk_ref, l_scr, a_scr = refs[8:]
        for i in range(4):
            l_scr[i * batch : (i + 1) * batch, :] = lgs[i][...]
            a_scr[i * batch : (i + 1) * batch, :qw] = acts[i][0]
            a_scr[i * batch : (i + 1) * batch, qw:] = acts[i][1]
        bias_sum = jnp.sum(a_scr[:, :qw].astype(f32), axis=0, keepdims=True)
        rows = [bias_sum[:, i * E : (i + 1) * E] for i in range(bq)]
        extra = jnp.concatenate(rows + [jnp.zeros((r - bq, E), f32)], axis=0).astype(bf)
        gu = _dot(l_scr[:, :rank], a_scr[:, :qw], 0, 0).astype(bf)
        gd = _dot(l_scr[:, rank:], a_scr[:, qw:], 0, 0).astype(bf)
        for k in range(TZ):
            for j, (u_ref, d_ref) in enumerate(((uk_ref, dk_ref), (us_ref, ds_ref))):
                b = k * 2 + j
                u_ref[k, :, :qw] = gu[b * r : (b + 1) * r]
                u_ref[k, :, qw:] = extra
                d_ref[k] = gd[b * r : (b + 1) * r]

    us, uk, ds, dk = _call(
        shares,
        [((TZ, r, qw + E), bf)] * 2 + [((TZ, r, qw), bf)] * 2,
        scratch=[pltpu.VMEM((4 * batch, 2 * rank), bf), pltpu.VMEM((4 * batch, 2 * qw), bf)],
        flops=16 * batch * rank * qw,
        moved=16 * batch * (rank + qw),
        name="shares",
        mib=10,
    )(lg, lg_x, lg_c, lg_xc, kk, from_x, from_core, from_xc)

    def pair(*refs):
        keep_ref, got_ref = refs[:2]
        for k in range(TZ):
            s = keep_ref[k].astype(f32) + got_ref[k].astype(f32)
            refs[2 + k][...] = s.astype(bf)

    def reduced(send, keep, name):
        got = swap(send, j=1)
        w = keep.shape[2]
        zs = _call(pair, [((r, w), bf)] * TZ, moved=6 * TZ * r * w, name=name)(keep, got)
        return [zs[0]] + [swap(zs[k], k=k) for k in range(1, TZ)]

    ups = reduced(us, uk, "pair_up")
    downs = reduced(ds, dk, "pair_down")
    last = _up(2, 16)

    def total(terms):
        while len(terms) > 1:
            terms = [a + b for a, b in zip(terms[::2], terms[1::2])]
        return terms[0]

    def finish(*refs):
        o_ref = refs[-1]
        up = total([u[...].astype(f32) for u in refs[:TZ]])
        down = total([d[...].astype(f32) for d in refs[TZ : 2 * TZ]])
        o_ref[:r, :] = up[:, :qw].astype(bf)
        o_ref[r : 2 * r, :] = down.astype(bf)
        row = jnp.concatenate([up[i : i + 1, qw:] for i in range(bq)], axis=1)
        hi = row.astype(bf).astype(f32)
        tail = jnp.concatenate([hi, row - hi, jnp.zeros((last - 2, qw), f32)], axis=0)
        o_ref[2 * r :, :] = tail.astype(bf)

    (fin,) = _call(finish, [((2 * r + last, qw), bf)], moved=8 * r * qw * TZ, name="finish", mib=6)(
        *ups, *downs
    )
    fin_x = swap(fin, dx=1)
    fin_c = swap(fin, dc=1)
    fin_xc = swap(fin_x, dc=1)

    def spread(*refs):
        ins = refs[:4]
        gd_ref, gu_ref, gb_ref, scr = refs[4:]
        d = lax.axis_index("dense")
        for off, i_ref in zip((0, 2, 1, 3), ins):
            q = jnp.bitwise_xor(d, off)
            scr[:, pl.ds(pl.multiple_of(q * qw, E), qw)] = i_ref[...].astype(f32)
        gu_ref[...] = scr[:r, :width]
        gd_ref[...] = scr[r : 2 * r, :width]
        gb_ref[...] = scr[2 * r, :width] + scr[2 * r + 1, :width]

    gdown, gup_w, gbias = _call(
        spread,
        [((r, width), f32)] * 2 + [((width,), f32)],
        scratch=[pltpu.VMEM((2 * r + last, padw), f32)],
        moved=24 * r * width,
        name="spread",
        mib=8,
    )(fin, fin_x, fin_c, fin_xc)

    half = nrow // 2

    def scatter(*refs):
        z_refs, (y_ref, mt_ref, keep_ref, send_ref, sg, out) = refs[:TZ], refs[TZ:]
        for k in range(TZ):
            sg[(2 * k) * cp : (2 * k + 1) * cp, :] = z_refs[k][0]
            sg[(2 * k + 1) * cp : (2 * k + 2) * cp, :] = y_ref[k]
        out[...] = _dot(mt_ref[...], sg[...], 1, 0)
        c = lax.rem(lax.axis_index("dense"), 2)
        keep_ref[...] = out[pl.ds(pl.multiple_of(c * half, 8), half), :]
        send_ref[...] = out[pl.ds(pl.multiple_of((1 - c) * half, 8), half), :].astype(bf)

    t_keep, t_send = _call(
        scatter,
        [((half, E), f32), ((half, E), bf)],
        scratch=[pltpu.VMEM((ns, E), bf), pltpu.VMEM((nrow, E), f32)],
        flops=2 * nrow * ns * E,
        moved=2 * nrow * ns,
        name="scatter",
        mib=8,
    )(*bzr, byr, mt)
    t_half = (t_keep + swap(t_send, dc=1).astype(f32)).astype(bf)
    t_sum = t_half.astype(f32) + swap(t_half, dx=1).astype(f32)
    t_other = swap(t_sum, dc=1)
    gtable = jnp.where(
        core == 0,
        jnp.concatenate([t_sum, t_other], axis=0),
        jnp.concatenate([t_other, t_sum], axis=0),
    )
    return (crossed[None], gtable, gdense[None], gdown, gup_w, gbias)


def fits(sizes, args):
    T, D = sizes
    table, slot_rows, down_w, grad_out = args[0], args[1], args[5], args[8]
    batch, width = grad_out.shape[1:]
    cap = slot_rows.shape[1] // T
    return (
        D == 4
        and T >= 4
        and T & (T - 1) == 0
        and down_w.shape[0] % 16 == 0
        and batch == E
        and width % E == 0
        and table.shape[0] % E == 0
        and cap % 8 == 0
        and cap <= E
        and -(-(width // E) // D) <= down_w.shape[0]
    )


def solution(mesh):
    placed = (
        P("table", None),
        P("dense", "table", None),
        P("dense", "table", None),
        P("dense", "table"),
        P("dense", "table", None),
        P("table", None),
        P("table", None),
        P(),
        P("dense", "table", None),
    )
    sizes = (mesh.shape["table"], mesh.shape["dense"])

    def step(*args):
        return fast(sizes, *args) if fits(sizes, args) else local(*args)

    return jax.shard_map(
        step,
        mesh=mesh,
        in_specs=placed,
        out_specs=(
            P("dense", "table", None),
            P("table", None),
            P("dense", "table", None),
            P("table", None),
            P("table", None),
            P(),
        ),
        check_vma=False,
    )
```
